32 devices in a mesh: lon: 8 (over y, x, core), lat: 4 (over z).
Axes of the slice: x: 2, y: 2, z: 4, core: 2. Of those that a mesh axis runs over, the one named last changes fastest.
Arguments:
- ocean_state: float32 [4, 4, 512, 8192], P(None, None, 'lat', 'lon'), may hold values from -3 to 3
- depth_levels: int32 [512, 8192], P('lat', 'lon'), may hold values from 0 to 4
- vert_mix: float32 [4, 512, 8192], P(None, 'lat', 'lon'), may hold values from 0.1 to 4
- partner: int32 [8192], P('lon'), may hold values from 0 to 8191, as said below
- ice_velocity: float32 [2, 512, 8192], P(None, 'lat', 'lon'), may hold values from -4 to 4
- ice_mass: float32 [512, 8192], P('lat', 'lon'), may hold values from 0.2 to 2
- ice_strength: float32 [512, 8192], P('lat', 'lon'), may hold values from 0.2 to 2
- ice_mask: int32 [512, 8192], P('lat', 'lon'), may hold values 0 or 1
- ice_owned: int32 [4, 8, 3], P('lat', 'lon'), may hold values from -1 to 63, as said below
Outputs:
- new_tracers: float32 [2, 4, 512, 8192], P(None, None, 'lat', 'lon')
- new_ice_velocity: float32 [2, 512, 8192], P(None, 'lat', 'lon')
The draws below stay inside these ranges and needn't reach their ends.
Inputs may be any that keep to these rules, and one draw needn't show every extreme that they name: partner[i] = (s - i) mod 8192 for one s drawn afresh; the partner of a column's partner is the column itself. `ice_owned`: entry [r, d, k] is -1 or a tile column of tile row r that lies on lon index (d - k) mod 8, that is, one of the 8 tile columns from ((d - k) mod 8) * 8 on; each tile column appears at most once in a row; in every row some lon index has all 3 slots filled and some lon index has none.
All inputs are finite; a program needn't handle non-finite values. No bound on the sum of `ice_mask` on one device may be relied on, other than what follows from the above.
Results may differ from the reference program's by a relative error of at most 0.0003.
Values sent between devices are 32-bit elements; how exact they have to be, the bound alone decides.
No kernel may reach another device: no remote copies, remote signals or barrier semaphores. Data moves between devices by JAX's collectives and lax.ppermute only.
A program may use at most 192 MiB of HBM per device.

```python
import math
import jax
import jax.numpy as jnp
from jax import lax

LEV = 4
TILE = 128
CX = 1024
OWN_MOST = 3
SUBCYCLES = 32
NY = 512
NX = 8192
N_LON = 8


def draw_partner(key, part):
    offset = jax.random.randint(key, (), 0, NX)
    return jnp.mod(offset - jnp.arange(NX, dtype=jnp.int32), NX).astype(jnp.int32)


def draw_ice_owned(key, part):
    tile_rows = NY // TILE
    tiles_dev = CX // TILE

    def one_row(row_key):
        sub_keys = jax.random.split(row_key, 4)
        start = jax.random.randint(sub_keys[0], (), 0, N_LON)
        run_length = jax.random.randint(sub_keys[1], (), OWN_MOST, N_LON // 2 + 1)
        orders = jax.vmap(lambda one_key: jax.random.permutation(one_key, tiles_dev).astype(jnp.int32))(jax.random.split(sub_keys[2], N_LON))
        owner_ids = jnp.arange(N_LON, dtype=jnp.int32)[:, None]
        slot_ids = jnp.arange(OWN_MOST, dtype=jnp.int32)[None, :]
        source = jnp.mod(owner_ids - slot_ids, N_LON)
        picked = jnp.take_along_axis(orders[:, :OWN_MOST], jnp.broadcast_to(slot_ids, (N_LON, OWN_MOST)), axis=1)
        local_pick = jnp.stack([picked[source[:, slot_id], slot_id] for slot_id in range(OWN_MOST)], axis=1)
        columns = source * tiles_dev + local_pick
        in_run = jnp.mod(source - start, N_LON) < run_length
        kept = in_run & (jax.random.randint(sub_keys[3], (N_LON, OWN_MOST), 0, 4) < 3)
        forced = jnp.mod(start + OWN_MOST - 1, N_LON)
        kept = kept | (owner_ids == forced) & in_run
        return jnp.where(kept, columns, -1).astype(jnp.int32)
    return jax.vmap(one_row)(jax.random.split(key, tile_rows)).astype(jnp.int32)


def place_ends(values, rng, least, top_value):
    shape = values.shape
    index_at = [jax.random.randint(jax.random.fold_in(rng, axis), (), 0, shape[axis]) for axis in range(len(shape))]
    values = values.at[tuple(index_at)].set(least)
    longest = shape.index(max(shape))
    index_at[longest] = (index_at[longest] + 1) % shape[longest]
    return values.at[tuple(index_at)].set(top_value)


def block_scale(own_key, dims, pieces, smallest, largest):
    level, own = 1.0, jax.random.fold_in(own_key, 6)
    for axis_at, parts in pieces:
        heights = jnp.exp(jax.random.uniform(jax.random.fold_in(own, axis_at), (parts,), jnp.float32, smallest / len(pieces), largest / len(pieces)))
        level = level * jnp.repeat(heights, dims[axis_at] // parts).reshape([-1 if axis == axis_at else 1 for axis in range(len(dims))])
    return level


def noise(key, dims, deviation, bound, pieces=(), kind=jnp.bfloat16):
    drawn = deviation * jax.random.normal(key, dims, jnp.float32)
    if pieces:
        drawn = drawn * block_scale(key, dims, pieces, -0.22, 0.18)
    return jnp.clip(drawn, -bound, bound).astype(kind)


def setup_inputs(seed: int = 0) -> dict:
    seeds = jax.random.split(jax.random.key(seed), 10)
    return {
        "ocean_state": noise(seeds[0], (4, LEV, NY, NX), 1.0, 3.0, ((2, 4), (3, 8)), jnp.float32),
        "depth_levels": place_ends(jax.random.randint(seeds[1], (NY, NX), 0, LEV + 1), jax.random.fold_in(seeds[1], 1), 0, LEV).astype(jnp.int32),
        "vert_mix": jnp.clip(jnp.exp(math.log(4.0) - 3.6888794 * jax.random.uniform(seeds[2], (LEV, NY, NX), jnp.float32) ** block_scale(seeds[2], (LEV, NY, NX), ((1, 4), (2, 8)), -0.2, 0.2)), 0.1, 4.0),
        "partner": draw_partner(jax.random.fold_in(seeds[9], 71), 0),
        "ice_velocity": noise(seeds[4], (2, NY, NX), 1.0, 4.0, ((1, 4), (2, 8)), jnp.float32),
        "ice_mass": jnp.clip(jnp.exp(math.log(2.0) - 2.3025851 * jax.random.uniform(seeds[5], (NY, NX), jnp.float32) ** block_scale(seeds[5], (NY, NX), ((0, 4), (1, 8)), -0.2, 0.2)), 0.2, 2.0),
        "ice_strength": jnp.clip(jnp.exp(math.log(2.0) - 2.3025851 * jax.random.uniform(seeds[6], (NY, NX), jnp.float32) ** block_scale(seeds[6], (NY, NX), ((0, 4), (1, 8)), -0.2, 0.2)), 0.2, 2.0),
        "ice_mask": place_ends((jax.random.randint(seeds[7], (NY, NX), 0, 4) < 3).astype(jnp.int32), jax.random.fold_in(seeds[7], 1), 0, 1),
        "ice_owned": draw_ice_owned(jax.random.fold_in(seeds[9], 71), 0),
    }


TIME_STEP = 0.25
MIX_HORIZ = 0.5
RELAX_RATE = 0.5
ECC_FACTOR = 0.25
DELTA_FLOOR_SQ = 0.25
INV_ICE_STEP = 2.0
WATER_DRAG = 1.0
CORIOLIS_PARAM = 0.5

def shift_ahead(values, which_dim):
    if which_dim == -1:
        return jnp.concatenate([values[..., 1:], jnp.zeros_like(values[..., :1])], axis=-1)
    return jnp.concatenate([values[..., 1:, :], jnp.zeros_like(values[..., :1, :])], axis=-2)

def shift_behind(values, which_dim):
    if which_dim == -1:
        return jnp.concatenate([jnp.zeros_like(values[..., :1]), values[..., :-1]], axis=-1)
    return jnp.concatenate([jnp.zeros_like(values[..., :1, :]), values[..., :-1, :]], axis=-2)

def ice_subcycles(vel_east, vel_north, mass_ice, strength, ocean_east, ocean_north):
    inertia = mass_ice * INV_ICE_STEP
    diag_coef = inertia + WATER_DRAG
    turning = CORIOLIS_PARAM * mass_ice
    denominator = diag_coef * diag_coef + turning * turning

    def one_cycle(cycle_id, carry):
        vel_east, vel_north, stress_sum, stress_diff, stress_shear = carry
        grad_east_u = shift_ahead(vel_east, -1) - vel_east
        grad_north_v = shift_ahead(vel_north, -2) - vel_north
        grad_north_u = shift_ahead(vel_east, -2) - vel_east
        grad_east_v = shift_ahead(vel_north, -1) - vel_north
        divergence = grad_east_u + grad_north_v
        tension = grad_east_u - grad_north_v
        shearing = grad_north_u + grad_east_v
        deform = jnp.sqrt(divergence * divergence + ECC_FACTOR * (tension * tension + shearing * shearing) + DELTA_FLOOR_SQ)
        pressure_ratio = strength / deform
        stress_sum = (stress_sum + RELAX_RATE * (pressure_ratio * divergence - strength)) / (1.0 + RELAX_RATE)
        stress_diff = (stress_diff + RELAX_RATE * ECC_FACTOR * pressure_ratio * tension) / (1.0 + RELAX_RATE)
        stress_shear = (stress_shear + RELAX_RATE * ECC_FACTOR * pressure_ratio * shearing) / (1.0 + RELAX_RATE)
        stress_xx = 0.5 * (stress_sum + stress_diff)
        stress_yy = 0.5 * (stress_sum - stress_diff)
        force_east = stress_xx - shift_behind(stress_xx, -1) + stress_shear - shift_behind(stress_shear, -2)
        force_north = stress_shear - shift_behind(stress_shear, -1) + stress_yy - shift_behind(stress_yy, -2)
        rhs_east = inertia * vel_east + force_east + WATER_DRAG * ocean_east
        rhs_north = inertia * vel_north + force_north + WATER_DRAG * ocean_north
        new_east = (diag_coef * rhs_east + turning * rhs_north) / denominator
        new_north = (diag_coef * rhs_north - turning * rhs_east) / denominator
        return (new_east, new_north, stress_sum, stress_diff, stress_shear)
    zeros = jnp.zeros_like(vel_east)
    result = lax.fori_loop(0, SUBCYCLES, one_cycle, (vel_east, vel_north, zeros, zeros, zeros))
    return (result[0], result[1])

def ocean_update(tracer_pad, east_pad, north_pad, depth_pad, vert_mix):
    level_count = vert_mix.shape[0]
    level_ids = jnp.arange(level_count, dtype=jnp.float32)[:, None, None]
    wet_pad = (level_ids < depth_pad[None]).astype(jnp.float32)
    wet_here = wet_pad[:, 1:-1, 1:-1]
    open_east = wet_here * wet_pad[:, 1:-1, 2:]
    open_west = wet_here * wet_pad[:, 1:-1, :-2]
    open_north = wet_here * wet_pad[:, 2:, 1:-1]
    open_south = wet_here * wet_pad[:, :-2, 1:-1]
    centre = tracer_pad[:, :, 1:-1, 1:-1]
    east_val = tracer_pad[:, :, 1:-1, 2:]
    west_val = tracer_pad[:, :, 1:-1, :-2]
    north_val = tracer_pad[:, :, 2:, 1:-1]
    south_val = tracer_pad[:, :, :-2, 1:-1]
    vel_east = east_pad[:, 1:-1, 1:-1]
    vel_west_face = east_pad[:, 1:-1, :-2]
    vel_north = north_pad[:, 1:-1, 1:-1]
    vel_south_face = north_pad[:, :-2, 1:-1]
    flux_east = (jnp.maximum(vel_east, 0.0) * centre + jnp.minimum(vel_east, 0.0) * east_val) * open_east
    flux_west = (jnp.maximum(vel_west_face, 0.0) * west_val + jnp.minimum(vel_west_face, 0.0) * centre) * open_west
    flux_north = (jnp.maximum(vel_north, 0.0) * centre + jnp.minimum(vel_north, 0.0) * north_val) * open_north
    flux_south = (jnp.maximum(vel_south_face, 0.0) * south_val + jnp.minimum(vel_south_face, 0.0) * centre) * open_south
    laplace = open_east * (east_val - centre) + open_west * (west_val - centre) + open_north * (north_val - centre) + open_south * (south_val - centre)
    interim = centre + TIME_STEP * (MIX_HORIZ * laplace - (flux_east - flux_west + flux_north - flux_south))
    coupling = [None] + [TIME_STEP * vert_mix[level_id] * wet_here[level_id] for level_id in range(1, level_count)]
    surface = TIME_STEP * vert_mix[0] * wet_here[0]
    upper_mod = []
    rhs_mod = []
    for level_id in range(level_count):
        diagonal = 1.0 + (surface if level_id == 0 else coupling[level_id])
        if level_id + 1 < level_count:
            diagonal = diagonal + coupling[level_id + 1]
        rhs_now = interim[:, level_id]
        if level_id > 0:
            lower_coef = -coupling[level_id]
            diagonal = diagonal - lower_coef * upper_mod[level_id - 1]
            rhs_now = rhs_now - lower_coef * rhs_mod[level_id - 1]
        if level_id + 1 < level_count:
            upper_mod.append(-coupling[level_id + 1] / diagonal)
        else:
            upper_mod.append(None)
        rhs_mod.append(rhs_now / diagonal)
    solved = [None] * level_count
    solved[level_count - 1] = rhs_mod[level_count - 1]
    for level_id in range(level_count - 2, -1, -1):
        solved[level_id] = rhs_mod[level_id] - upper_mod[level_id] * solved[level_id + 1]
    return jnp.stack(solved, axis=1)

def pad_grid(values, partner):
    north_row = jnp.take(values[..., -1:, :], partner, axis=-1)
    south_row = jnp.zeros_like(values[..., :1, :])
    extended = jnp.concatenate([south_row, values, north_row], axis=-2)
    return jnp.concatenate([extended[..., -1:], extended, extended[..., :1]], axis=-1)

def reference(ocean_state, depth_levels, vert_mix, partner, ice_velocity, ice_mass, ice_strength, ice_mask, ice_owned):
    depths = depth_levels.astype(jnp.float32)
    padded_state = pad_grid(ocean_state, partner)
    depth_pad = pad_grid(depths, partner)
    new_tracers = ocean_update(padded_state[0:2], padded_state[2], padded_state[3], depth_pad, vert_mix)
    ice_cover = ice_mask.astype(jnp.float32) * (depth_levels > 0).astype(jnp.float32)
    tile_rows = NY // TILE
    tile_cols = NX // TILE

    def to_tiles(values):
        return values.reshape(tile_rows, TILE, tile_cols, TILE).transpose(0, 2, 1, 3)

    def from_tiles(values):
        return values.transpose(0, 2, 1, 3).reshape(NY, NX)
    old_east = to_tiles(ice_velocity[0])
    old_north = to_tiles(ice_velocity[1])
    new_east, new_north = ice_subcycles(old_east, old_north, to_tiles(ice_mass * ice_cover), to_tiles(ice_strength * ice_cover), to_tiles(ocean_state[2, 0]), to_tiles(ocean_state[3, 0]))
    listed = jnp.any(ice_owned[:, :, :, None] == jnp.arange(tile_cols, dtype=jnp.int32)[None, None, None, :], axis=(1, 2))
    east_out = jnp.where(listed[:, :, None, None], new_east, old_east)
    north_out = jnp.where(listed[:, :, None, None], new_north, old_north)
    return (new_tracers, jnp.stack([from_tiles(east_out), from_tiles(north_out)]))
```

```python
import functools

import jax
import jax.numpy as jnp
from jax import lax
from jax.experimental import pallas as pl
from jax.experimental.pallas import tpu as pltpu
from jax.sharding import PartitionSpec as P

TILE = 128
SUBCYCLES = 32
LANES = 128
SUB = 8

TIME_STEP = 0.25
MIX_HORIZ = 0.5
RELAX_RATE = 0.5
ECC_FACTOR = 0.25
DELTA_FLOOR_SQ = 0.25
INV_ICE_STEP = 2.0
WATER_DRAG = 1.0
CORIOLIS_PARAM = 0.5

f32 = jnp.float32
ANY = pl.BlockSpec(memory_space=pl.ANY)
SMEM_SPEC = pl.BlockSpec(memory_space=pltpu.SMEM)


def lane_ids():
    return lax.broadcasted_iota(jnp.int32, (SUB, LANES), 1)


def sub_ids():
    return lax.broadcasted_iota(jnp.int32, (SUB, LANES), 0)


def east_of(cur, nxt, lane0):
    return pltpu.roll(jnp.where(lane0, nxt, cur), LANES - 1, 1)


def west_of(cur, prev, lane_last):
    return pltpu.roll(jnp.where(lane_last, prev, cur), 1, 1)


def north_of(cur, nxt, sub0):
    return pltpu.roll(jnp.where(sub0, nxt, cur), SUB - 1, 0)


def south_of(cur, prev, sub_last):
    return pltpu.roll(jnp.where(sub_last, prev, cur), 1, 0)


N_VEC = TILE // SUB


def ice_tile(fields, mask_ref, depth_ref, st, cf):
    lane, sub = lane_ids(), sub_ids()
    lane_first, lane_last = lane == 0, lane == LANES - 1
    sub_first, sub_last = sub == 0, sub == SUB - 1
    zero = jnp.zeros((SUB, LANES), f32)

    def rows(ref, index, v):
        return ref[index, pl.ds(v, SUB, stride=N_VEC), :]

    def ahead_lane(x):
        return jnp.where(lane_last, zero, pltpu.roll(x, LANES - 1, 1))

    def behind_lane(x):
        return jnp.where(lane_first, zero, pltpu.roll(x, 1, 1))

    def ahead_wrap(x):
        return jnp.where(sub_last, zero, pltpu.roll(x, SUB - 1, 0))

    def behind_wrap(x):
        return jnp.where(sub_first, zero, pltpu.roll(x, 1, 0))

    half_p = []
    for v in range(N_VEC):
        ice = mask_ref[pl.ds(v, SUB, stride=N_VEC), :].astype(f32)
        wet = depth_ref[pl.ds(v, SUB, stride=N_VEC), :] > 0
        cover = jnp.where(wet, ice, zero)
        mass = rows(fields, 2, v) * cover
        strength = rows(fields, 3, v) * cover
        inertia = mass * INV_ICE_STEP
        diag = inertia + WATER_DRAG
        turn = CORIOLIS_PARAM * mass
        inv = 1.0 / (diag * diag + turn * turn)
        half = 0.5 * strength
        half_p.append(half)
        st[0, v] = rows(fields, 0, v)
        st[1, v] = rows(fields, 1, v)
        st[2, v] = half
        st[3, v] = half
        st[4, v] = zero
        cf[0, v] = strength * (1.0 / 12.0)
        cf[1, v] = inertia
        cf[2, v] = diag * inv
        cf[3, v] = turn * inv
    for v in range(N_VEC):
        half = half_p[v]
        below = half_p[v - 1] if v else behind_wrap(half_p[N_VEC - 1])
        cf[4, v] = WATER_DRAG * rows(fields, 4, v) - (half - behind_lane(half))
        cf[5, v] = WATER_DRAG * rows(fields, 5, v) - (half - below)

    keep = 1.0 / (1.0 + RELAX_RATE)

    def one_cycle(_, carry):
        def update(v, u, w, sxx, syy, s12, syy_below, s12_below):
            fx = (sxx - behind_lane(sxx)) + (s12 - s12_below)
            fy = (s12 - behind_lane(s12)) + (syy - syy_below)
            inertia, ca, cb = cf[1, v], cf[2, v], cf[3, v]
            rx = inertia * u + (fx + cf[4, v])
            ry = inertia * w + (fy + cf[5, v])
            st[0, v] = ca * rx + cb * ry
            st[1, v] = ca * ry - cb * rx

        u, w = st[0, 0], st[1, 0]
        first_u, first_w = u, w
        first = prev = None
        for v in range(N_VEC):
            if v + 1 < N_VEC:
                u_north, w_north = st[0, v + 1], st[1, v + 1]
            else:
                u_north, w_north = ahead_wrap(first_u), ahead_wrap(first_w)
            ux = ahead_lane(u) - u
            vy = w_north - w
            shear = (u_north - u) + (ahead_lane(w) - w)
            div = ux + vy
            tens = ux - vy
            div2 = div + div
            four = div2 * div2 + (tens * tens + (shear * shear + 4.0 * DELTA_FLOOR_SQ))
            k = cf[0, v] * lax.rsqrt(four)
            div4 = div2 + div2
            sxx = keep * st[2, v] + k * (div4 + tens)
            syy = keep * st[3, v] + k * (div4 - tens)
            s12 = keep * st[4, v] + (k + k) * shear
            st[2, v] = sxx
            st[3, v] = syy
            st[4, v] = s12
            if v == 0:
                first = (sxx, syy, s12)
            else:
                update(v, u, w, sxx, syy, s12, prev[1], prev[2])
            prev = (sxx, syy, s12)
            u, w = u_north, w_north
        update(0, first_u, first_w, *first, behind_wrap(prev[1]), behind_wrap(prev[2]))
        return carry

    lax.fori_loop(0, SUBCYCLES, one_cycle, 0)
    for v in range(N_VEC):
        fields[0, pl.ds(v, SUB, stride=N_VEC), :] = st[0, v]
        fields[1, pl.ds(v, SUB, stride=N_VEC), :] = st[1, v]


def tile_copies(col, refs, fields, mask_v, depth_v, sems):
    vel, mass, strength, mask, depth, ocean = refs
    levels = ocean.shape[0] // 4
    cols = pl.ds(pl.multiple_of(col * TILE, TILE), TILE)
    return [
        pltpu.make_async_copy(vel.at[:, :, cols], fields.at[0:2], sems.at[0]),
        pltpu.make_async_copy(mass.at[:, cols], fields.at[2], sems.at[1]),
        pltpu.make_async_copy(strength.at[:, cols], fields.at[3], sems.at[2]),
        pltpu.make_async_copy(ocean.at[2 * levels, :, cols], fields.at[4], sems.at[3]),
        pltpu.make_async_copy(ocean.at[3 * levels, :, cols], fields.at[5], sems.at[4]),
        pltpu.make_async_copy(mask.at[:, cols], mask_v, sems.at[5]),
        pltpu.make_async_copy(depth.at[:, cols], depth_v, sems.at[6]),
    ]


TILE_COPIES = 7


def ice_scratch():
    return [
        pltpu.VMEM((6, TILE, TILE), f32),
        pltpu.VMEM((TILE, TILE), jnp.int32),
        pltpu.VMEM((TILE, TILE), jnp.int32),
        pltpu.SemaphoreType.DMA((TILE_COPIES,)),
    ]


def first_ice_kernel(
    owned, vel, mass, strength, mask, depth, ocean, out,
    fields, mask_v, depth_v, sems, st, cf, all_vel, copy_sems, all_sem,
):
    tiles_dev = vel.shape[2] // TILE
    column = owned[0, 0, 0]
    listed = column >= 0
    local = jnp.where(listed, column - lax.axis_index("lon") * tiles_dev, -1)
    safe = jnp.clip(local, 0, tiles_dev - 1)
    refs = (vel, mass, strength, mask, depth, ocean)
    whole = pltpu.make_async_copy(vel, all_vel, all_sem)

    def pass_through(q):
        cols = pl.ds(q * TILE, TILE)
        return pltpu.make_async_copy(all_vel.at[:, :, cols], out.at[:, :, cols], copy_sems.at[q])

    @pl.when(listed)
    def _():
        for copy in tile_copies(safe, refs, fields, mask_v, depth_v, sems):
            copy.start()

    whole.start()
    whole.wait()
    for q in range(tiles_dev):

        @pl.when(local != q)
        def _():
            pass_through(q).start()

    @pl.when(listed)
    def _():
        for copy in tile_copies(safe, refs, fields, mask_v, depth_v, sems):
            copy.wait()
        ice_tile(fields, mask_v, depth_v, st, cf)
        cols = pl.ds(pl.multiple_of(safe * TILE, TILE), TILE)
        back = pltpu.make_async_copy(fields.at[0:2], out.at[:, :, cols], sems.at[0])
        back.start()
        back.wait()

    for q in range(tiles_dev):

        @pl.when(local != q)
        def _():
            pass_through(q).wait()


def first_ice(owned, vel, mass, strength, mask, depth, ocean):
    return pl.pallas_call(
        first_ice_kernel,
        out_shape=jax.ShapeDtypeStruct(vel.shape, f32),
        in_specs=[SMEM_SPEC] + [ANY] * 6,
        out_specs=ANY,
        scratch_shapes=ice_scratch()
        + [
            pltpu.VMEM((5, N_VEC, SUB, LANES), f32),
            pltpu.VMEM((6, N_VEC, SUB, LANES), f32),
            pltpu.VMEM(vel.shape, f32),
            pltpu.SemaphoreType.DMA((vel.shape[2] // TILE,)),
            pltpu.SemaphoreType.DMA,
        ],
        name="ice_first",
    )(owned, vel, mass, strength, mask, depth, ocean)


class Layout:
    def __init__(self, ocean, rows, cols):
        self.levels = ocean // 4
        self.planes = 2 * self.levels
        self.tiles = cols // LANES
        self.fold_depth = self.tiles * self.planes
        self.columns = self.fold_depth + self.tiles
        self.column_fields = self.planes + self.levels + 1
        self.owned = self.columns + 16
        self.size = self.owned + SUB
        self.row_fields = 16


def pack_kernel(
    lay, owned, ocean, depth, piece_out, up_out, down_out, top, top_d, bot, bot_d, west, west_d, east, east_d, tmp, sems
):
    planes, levels, tiles = lay.planes, lay.levels, lay.tiles
    rows, cols = ocean.shape[1], ocean.shape[2]
    n_lon = piece_out.shape[0]
    me = lax.axis_index("lon")
    last = pl.ds(rows - SUB, SUB)
    copies = [
        pltpu.make_async_copy(ocean.at[0:planes, :, 0:LANES], west, sems.at[0]),
        pltpu.make_async_copy(ocean.at[0 : planes + levels, :, cols - LANES : cols], east, sems.at[1]),
        pltpu.make_async_copy(depth.at[:, 0:LANES], west_d, sems.at[2]),
        pltpu.make_async_copy(depth.at[:, cols - LANES : cols], east_d, sems.at[3]),
        pltpu.make_async_copy(ocean.at[:, last, :], top, sems.at[4]),
        pltpu.make_async_copy(depth.at[last, :], top_d, sems.at[5]),
        pltpu.make_async_copy(ocean.at[0:planes, 0:SUB, :], bot, sems.at[6]),
        pltpu.make_async_copy(depth.at[0:SUB, :], bot_d, sems.at[7]),
    ]
    for copy in copies:
        copy.start()
    for copy in copies[:4]:
        copy.wait()
    lane = lane_ids()
    for v in range(rows // SUB):
        at = pl.ds(v * SUB, SUB)
        mixed = jnp.zeros((SUB, LANES), f32)
        for f in range(planes + levels + 1):
            block = east[f, at, :] if f < planes + levels else east_d[at, :].astype(f32)
            mixed = jnp.where(lane == f, pltpu.roll(block, (f + 1) % LANES, 1), mixed)
        for f in range(planes + 1):
            block = west[f, at, :] if f < planes else west_d[at, :].astype(f32)
            mixed = jnp.where(lane == 16 + f, pltpu.roll(block, 16 + f, 1), mixed)
        tmp[at, :] = mixed
    turned = jnp.transpose(tmp[...])
    east_rows, west_rows = turned[0:16], turned[16:32]
    own = jnp.zeros((SUB, LANES), f32)
    for slot in range(owned.shape[2]):
        own = jnp.where(lane == slot, owned[0, 0, slot].astype(f32), own)
    for copy in copies[4:]:
        copy.wait()
    top_rows = jnp.concatenate([top[p, SUB - 1 : SUB, :] for p in range(planes)], axis=0)
    bot_rows = jnp.concatenate([bot[p, 0:1, :] for p in range(planes)], axis=0)
    top_depth = top_d[SUB - 1 : SUB, :].astype(f32)
    up_out[0:planes, :] = top_rows
    for level in range(levels):
        up_out[planes + level : planes + level + 1, :] = top[planes + levels + level, SUB - 1 : SUB, :]
    up_out[planes + levels : planes + levels + 1, :] = top_depth
    down_out[0:planes, :] = bot_rows
    down_out[planes : planes + 1, :] = bot_d[0:1, :].astype(f32)
    for d in range(n_lon):
        for t in range(tiles):
            at = slice(t * LANES, (t + 1) * LANES)
            piece_out[d, t * planes : (t + 1) * planes, :] = top_rows[:, at]
            piece_out[d, lay.fold_depth + t : lay.fold_depth + t + 1, :] = top_depth[:, at]
        eastward = d == lax.rem(me + 1, n_lon)
        piece_out[d, lay.columns : lay.columns + 16, :] = jnp.where(eastward, east_rows, west_rows)
        piece_out[d, lay.owned : lay.owned + SUB, :] = own


def pack(lay, n_lon, owned, ocean, depth):
    rows, cols = ocean.shape[1:]
    full = pl.BlockSpec(memory_space=pltpu.VMEM)
    return pl.pallas_call(
        functools.partial(pack_kernel, lay),
        out_shape=(
            jax.ShapeDtypeStruct((n_lon, lay.size, LANES), f32),
            jax.ShapeDtypeStruct((lay.row_fields, cols), f32),
            jax.ShapeDtypeStruct((lay.row_fields, cols), f32),
        ),
        in_specs=[SMEM_SPEC, ANY, ANY],
        out_specs=(full, full, full),
        scratch_shapes=[
            pltpu.VMEM((4 * lay.levels, SUB, cols), f32),
            pltpu.VMEM((SUB, cols), jnp.int32),
            pltpu.VMEM((lay.planes, SUB, cols), f32),
            pltpu.VMEM((SUB, cols), jnp.int32),
            pltpu.VMEM((lay.planes, rows, LANES), f32),
            pltpu.VMEM((rows, LANES), jnp.int32),
            pltpu.VMEM((lay.planes + lay.levels, rows, LANES), f32),
            pltpu.VMEM((rows, LANES), jnp.int32),
            pltpu.VMEM((rows, LANES), f32),
            pltpu.SemaphoreType.DMA((8,)),
        ],
        name="pack",
    )(owned, ocean, depth)


def face(lower, upper, vel, shut_above, level):
    quarter = TIME_STEP * vel
    away = jnp.maximum(quarter, 0.0) + TIME_STEP * MIX_HORIZ
    back = quarter - away
    is_open = float(level) < shut_above
    zero = jnp.zeros((SUB, LANES), f32)
    away = jnp.where(is_open, away, zero)
    back = jnp.where(is_open, back, zero)
    return [away * a + back * b for a, b in zip(lower, upper, strict=True)]


def main_kernel(
    lay, n_lon, n_lat, slots,
    partner, ocean, depth, vert, got, from_south, from_north,
    vel, mass, strength, mask, vel_alias,
    out, ice_out,
    cbuf, ubuf, vbuf, mbuf, dint, dbuf, obuf, fold, sides, lists, hal_e, hal_w, gprev, ndep,
    fields, mask_v, depth_v, tile_sems, st, cf, in_sems, out_sems, list_sems, got_sems,
):
    planes, levels, tiles = lay.planes, lay.levels, lay.tiles
    rows, cols = depth.shape
    blocks = rows // SUB
    me, row_at = lax.axis_index("lon"), lax.axis_index("lat")
    tiles_dev = cols // TILE
    east_dev, west_dev = lax.rem(me + 1, n_lon), lax.rem(me + n_lon - 1, n_lon)

    list_copies = [
        pltpu.make_async_copy(
            got.at[lax.rem(me + slot, n_lon), pl.ds(lay.owned, SUB), :], lists.at[slot - 1], list_sems.at[slot - 1]
        )
        for slot in range(1, slots)
    ]
    for copy in list_copies:
        copy.start()
    start = partner[0]
    source = start // cols
    before = lax.rem(source + n_lon - 1, n_lon)
    got_copies = [
        pltpu.make_async_copy(got.at[source], fold.at[1], got_sems.at[0]),
        pltpu.make_async_copy(got.at[before], fold.at[0], got_sems.at[1]),
        pltpu.make_async_copy(got.at[east_dev, pl.ds(lay.columns, 16), :], sides.at[0], got_sems.at[2]),
        pltpu.make_async_copy(got.at[west_dev, pl.ds(lay.columns, 16), :], sides.at[1], got_sems.at[3]),
    ]
    in_copies = [
        pltpu.make_async_copy(depth, dint, in_sems.at[0]),
        pltpu.make_async_copy(ocean.at[0:planes], cbuf.at[:, 0:rows, :], in_sems.at[1]),
        pltpu.make_async_copy(ocean.at[planes : planes + levels], ubuf, in_sems.at[2]),
        pltpu.make_async_copy(ocean.at[planes + levels : planes + 2 * levels], vbuf, in_sems.at[3]),
        pltpu.make_async_copy(vert, mbuf, in_sems.at[4]),
    ]
    tile_refs = (vel, mass, strength, mask, depth, ocean)
    for copy in list_copies:
        copy.wait()
    listed, local = [], []
    for slot in range(1, slots):
        column = lists[slot - 1, 0, slot].astype(jnp.int32)
        listed.append(column >= 0)
        local.append(jnp.clip(column - me * tiles_dev, 0, tiles_dev - 1))
    for slot in range(1, slots):

        @pl.when(listed[slot - 1])
        def _():
            for copy in tile_copies(
                local[slot - 1], tile_refs, fields.at[slot - 1], mask_v.at[slot - 1], depth_v.at[slot - 1],
                tile_sems.at[slot - 1],
            ):
                copy.start()

    for copy in got_copies + in_copies:
        copy.start()

    def write_back(slot):
        cols_at = pl.ds(pl.multiple_of(local[slot - 1] * TILE, TILE), TILE)
        return pltpu.make_async_copy(
            fields.at[slot - 1, 0:2], ice_out.at[:, :, cols_at], tile_sems.at[slot - 1, 0]
        )

    for slot in range(1, slots):

        @pl.when(listed[slot - 1])
        def _():
            for copy in tile_copies(
                local[slot - 1], tile_refs, fields.at[slot - 1], mask_v.at[slot - 1], depth_v.at[slot - 1],
                tile_sems.at[slot - 1],
            ):
                copy.wait()
            ice_tile(fields.at[slot - 1], mask_v.at[slot - 1], depth_v.at[slot - 1], st, cf)
            write_back(slot).start()

    lane, sub = lane_ids(), sub_ids()
    lane0, lane_last = lane == 0, lane == LANES - 1
    sub0, sub_last = sub == 0, sub == SUB - 1

    for copy in got_copies:
        copy.wait()
    pad = jnp.zeros((LANES - 16, LANES), f32)
    hal_e[...] = jnp.transpose(jnp.concatenate([sides[0], pad], axis=0))
    hal_w[...] = jnp.transpose(jnp.concatenate([sides[1], pad], axis=0))

    for copy in in_copies:
        copy.wait()

    at_top = row_at == n_lat - 1
    offset = lax.rem(start, cols)
    chunk, shift = offset // LANES, lax.rem(offset, LANES)
    index = lax.rem(shift - lane + LANES, LANES)
    from_upper = lane <= shift

    def fold_tile(pos, t):
        which, tile = pos // tiles, lax.rem(pos, tiles)
        tracers = fold[which, pl.ds(pl.multiple_of(tile * planes, SUB), planes), :]
        deep = fold[which, pl.ds(lay.fold_depth + tile, 1), :]
        return tracers, jnp.broadcast_to(deep, (SUB, LANES))

    for t in range(tiles):
        at = slice(t * LANES, (t + 1) * LANES)
        high, high_d = fold_tile(tiles + chunk - t, t)
        low, low_d = fold_tile(tiles + chunk - t - 1, t)
        def pick(a, b):
            return jnp.where(
                from_upper, jnp.take_along_axis(a, index, axis=1), jnp.take_along_axis(b, index, axis=1)
            )
        north = jnp.where(at_top, pick(high, low), from_north[0:planes, at])
        north_d = jnp.where(at_top, pick(high_d, low_d), from_north[planes : planes + 1, at])
        for p in range(planes):
            cbuf[p, rows : rows + SUB, at] = jnp.broadcast_to(north[p : p + 1], (SUB, LANES))
        dbuf[rows : rows + SUB, at] = north_d
    for b in range(blocks):
        dbuf[b * SUB : (b + 1) * SUB, :] = dint[b * SUB : (b + 1) * SUB, :].astype(f32)

    def tracers_of(level):
        return (level, levels + level)

    not_bottom = row_at > 0
    for t in range(tiles):
        at = slice(t * LANES, (t + 1) * LANES)
        deep = jnp.where(not_bottom, from_south[planes + levels : planes + levels + 1, at], 0.0)
        shut = jnp.minimum(jnp.broadcast_to(deep, (SUB, LANES)), north_of(dbuf[0:SUB, at], dbuf[0:SUB, at], sub0))
        for level in range(levels):
            lower = [jnp.broadcast_to(from_south[p : p + 1, at], (SUB, LANES)) for p in tracers_of(level)]
            upper = [north_of(cbuf[p, 0:SUB, at], cbuf[p, 0:SUB, at], sub0) for p in tracers_of(level)]
            speed = jnp.broadcast_to(from_south[planes + level : planes + level + 1, at], (SUB, LANES))
            for p, g in zip(tracers_of(level), face(lower, upper, speed, shut, level), strict=True):
                gprev[p, :, at] = g

    zero = jnp.zeros((SUB, LANES), f32)

    def one_block(b, carry):
        r0 = pl.multiple_of(b * SUB, SUB)
        here, ahead = pl.ds(r0, SUB), pl.ds(pl.multiple_of(r0 + SUB, SUB), SUB)
        side_e, side_w = hal_e[here, :], hal_w[here, :]

        def load_c(t):
            at = slice(t * LANES, (t + 1) * LANES)
            return [cbuf[p, here, at] for p in range(planes)]

        cur, cur_d = load_c(0), dbuf[here, 0:LANES]
        shut = jnp.minimum(pltpu.roll(side_w, (LANES - 1 - (planes + levels)) % LANES, 1), pltpu.roll(cur_d, LANES - 1, 1))
        g_prev = [None] * planes
        for level in range(levels):
            lower = [pltpu.roll(side_w, LANES - 1 - p, 1) for p in tracers_of(level)]
            upper = [pltpu.roll(cur[p], LANES - 1, 1) for p in tracers_of(level)]
            speed = pltpu.roll(side_w, LANES - 1 - (planes + level), 1)
            for p, g in zip(tracers_of(level), face(lower, upper, speed, shut, level), strict=True):
                g_prev[p] = g
        for t in range(tiles):
            at = slice(t * LANES, (t + 1) * LANES)
            if t + 1 < tiles:
                nxt, nxt_d = load_c(t + 1), dbuf[here, (t + 1) * LANES : (t + 2) * LANES]
            else:
                nxt = [pltpu.roll(side_e, (LANES - p) % LANES, 1) for p in range(planes)]
                nxt_d = pltpu.roll(side_e, LANES - planes, 1)
            shut_e = jnp.minimum(cur_d, east_of(cur_d, nxt_d, lane0))
            shut_n = jnp.minimum(cur_d, north_of(cur_d, dbuf[ahead, at], sub0))
            interim = [None] * planes
            for level in range(levels):
                pair = tracers_of(level)
                lower = [cur[p] for p in pair]
                east = [east_of(cur[p], nxt[p], lane0) for p in pair]
                north = [north_of(cur[p], cbuf[p, ahead, at], sub0) for p in pair]
                g_east = face(lower, east, ubuf[level, here, at], shut_e, level)
                g_north = face(lower, north, vbuf[level, here, at], shut_n, level)
                for p, c, ge, gn in zip(pair, lower, g_east, g_north, strict=True):
                    g_west = west_of(ge, g_prev[p], lane_last)
                    g_south = south_of(gn, gprev[p, :, at], sub_last)
                    gprev[p, :, at] = gn
                    g_prev[p] = ge
                    interim[p] = c - ((ge - g_west) + (gn - g_south))
            mix = [
                jnp.where(float(level) < cur_d, TIME_STEP * mbuf[level, here, at], zero) for level in range(levels)
            ]
            ratio = [None] * levels
            solved = [None] * planes
            y = [[None] * levels, [None] * levels]
            for level in range(levels):
                diag = mix[level] + 1.0
                if level + 1 < levels:
                    diag = diag + mix[level + 1]
                if level:
                    ratio[level] = mix[level] * inv
                    diag = diag - mix[level] * ratio[level]
                inv = 1.0 / diag
                for tracer in range(2):
                    rhs = interim[tracer * levels + level]
                    if level:
                        rhs = rhs + mix[level] * y[tracer][level - 1]
                    y[tracer][level] = rhs * inv
            for tracer in range(2):
                z = y[tracer][levels - 1]
                obuf[tracer * levels + levels - 1, here, at] = z
                for level in range(levels - 2, -1, -1):
                    z = y[tracer][level] + ratio[level + 1] * z
                    obuf[tracer * levels + level, here, at] = z
            cur, cur_d = nxt, nxt_d
        return carry

    parts = out_sems.shape[0]
    per = blocks // parts

    def out_copy(part):
        at = pl.ds(part * per * SUB, per * SUB)
        return pltpu.make_async_copy(obuf.at[:, at, :], out.at[:, at, :], out_sems.at[part])

    for part in range(parts):
        lax.fori_loop(part * per, (part + 1) * per, one_block, 0)
        out_copy(part).start()
    for slot in range(1, slots):

        @pl.when(listed[slot - 1])
        def _():
            write_back(slot).wait()

    for part in range(parts):
        out_copy(part).wait()


def main(lay, n_lon, n_lat, slots, partner, ocean, depth, vert, got, south, north, vel, mass, strength, mask, ice):
    rows, cols = depth.shape
    levels, planes = lay.levels, lay.planes
    full = pl.BlockSpec(memory_space=pltpu.VMEM)
    extra = slots - 1
    return pl.pallas_call(
        functools.partial(main_kernel, lay, n_lon, n_lat, slots),
        out_shape=(
            jax.ShapeDtypeStruct((planes, rows, cols), f32),
            jax.ShapeDtypeStruct(ice.shape, f32),
        ),
        in_specs=[SMEM_SPEC, ANY, ANY, ANY, ANY, full, full] + [ANY] * 5,
        out_specs=(ANY, ANY),
        input_output_aliases={11: 1},
        scratch_shapes=[
            pltpu.VMEM((planes, rows + SUB, cols), f32),
            pltpu.VMEM((levels, rows, cols), f32),
            pltpu.VMEM((levels, rows, cols), f32),
            pltpu.VMEM((levels, rows, cols), f32),
            pltpu.VMEM((rows, cols), jnp.int32),
            pltpu.VMEM((rows + SUB, cols), f32),
            pltpu.VMEM((planes, rows, cols), f32),
            pltpu.VMEM((2, lay.size, LANES), f32),
            pltpu.VMEM((2, 16, LANES), f32),
            pltpu.SMEM((extra, SUB, LANES), f32),
            pltpu.VMEM((rows, LANES), f32),
            pltpu.VMEM((rows, LANES), f32),
            pltpu.VMEM((planes, SUB, cols), f32),
            pltpu.VMEM((SUB, LANES), f32),
            pltpu.VMEM((extra, 6, TILE, TILE), f32),
            pltpu.VMEM((extra, TILE, TILE), jnp.int32),
            pltpu.VMEM((extra, TILE, TILE), jnp.int32),
            pltpu.SemaphoreType.DMA((extra, TILE_COPIES)),
            pltpu.VMEM((5, N_VEC, SUB, LANES), f32),
            pltpu.VMEM((6, N_VEC, SUB, LANES), f32),
            pltpu.SemaphoreType.DMA((5,)),
            pltpu.SemaphoreType.DMA((4,)),
            pltpu.SemaphoreType.DMA((extra,)),
            pltpu.SemaphoreType.DMA((4,)),
        ],
        name="main",
    )(partner, ocean, depth, vert, got, south, north, vel, mass, strength, mask, ice)


def on_device(
    ocean_state,
    depth_levels,
    vert_mix,
    partner,
    ice_velocity,
    ice_mass,
    ice_strength,
    ice_mask,
    ice_owned,
):
    n_lon, n_lat = lax.axis_size("lon"), lax.axis_size("lat")
    fields, levels, rows, cols = ocean_state.shape
    ocean = ocean_state.reshape(fields * levels, rows, cols)
    lay = Layout(fields * levels, rows, cols)
    piece, up, down = pack(lay, n_lon, ice_owned, ocean, depth_levels)
    got = lax.all_to_all(piece, "lon", 0, 0, tiled=True)
    south = lax.ppermute(up, "lat", [(i, i + 1) for i in range(n_lat - 1)])
    north = lax.ppermute(down, "lat", [(i + 1, i) for i in range(n_lat - 1)])
    ice = first_ice(ice_owned, ice_velocity, ice_mass, ice_strength, ice_mask, depth_levels, ocean)
    tracers, ice = main(
        lay, n_lon, n_lat, ice_owned.shape[2], partner, ocean, depth_levels, vert_mix, got, south, north,
        ice_velocity, ice_mass, ice_strength, ice_mask, ice,
    )
    return tracers.reshape(2, levels, rows, cols), ice


def solution(mesh):
    return jax.shard_map(
        on_device,
        mesh=mesh,
        in_specs=(
            P(None, None, "lat", "lon"),
            P("lat", "lon"),
            P(None, "lat", "lon"),
            P("lon"),
            P(None, "lat", "lon"),
            P("lat", "lon"),
            P("lat", "lon"),
            P("lat", "lon"),
            P("lat", "lon", None),
        ),
        out_specs=(P(None, None, "lat", "lon"), P(None, "lat", "lon")),
        check_vma=False,
    )
```

```python
import functools

import jax
import jax.numpy as jnp
from jax import lax
from jax.experimental import pallas as pl
from jax.experimental.pallas import tpu as pltpu
from jax.sharding import PartitionSpec as P

TILE = 128
SUBCYCLES = 32
LANES = 128
SUB = 8
MAIN_VMEM = 54_000_000
FIRST_VMEM = 54_000_000

TIME_STEP = 0.25
MIX_HORIZ = 0.5
RELAX_RATE = 0.5
ECC_FACTOR = 0.25
DELTA_FLOOR_SQ = 0.25
INV_ICE_STEP = 2.0
WATER_DRAG = 1.0
CORIOLIS_PARAM = 0.5

f32 = jnp.float32
ANY = pl.BlockSpec(memory_space=pltpu.HBM)
SMEM_SPEC = pl.BlockSpec(memory_space=pltpu.SMEM)


def lane_ids():
    return lax.broadcasted_iota(jnp.int32, (SUB, LANES), 1)


def sub_ids():
    return lax.broadcasted_iota(jnp.int32, (SUB, LANES), 0)


def east_of(cur, nxt, lane0):
    return pltpu.roll(jnp.where(lane0, nxt, cur), LANES - 1, 1)


def west_of(cur, prev, lane_last):
    return pltpu.roll(jnp.where(lane_last, prev, cur), 1, 1)


def north_of(cur, nxt, sub0):
    return pltpu.roll(jnp.where(sub0, nxt, cur), SUB - 1, 0)


def south_of(cur, prev, sub_last):
    return pltpu.roll(jnp.where(sub_last, prev, cur), 1, 0)


N_VEC = TILE // SUB


def ice_prepare(fields, mask_ref, depth_ref, st, cf):
    lane, sub = lane_ids(), sub_ids()
    zero = jnp.zeros((SUB, LANES), f32)

    def rows(ref, index, v):
        return ref[index, pl.ds(v, SUB, stride=N_VEC), :]

    half_p = []
    for v in range(N_VEC):
        ice = mask_ref[pl.ds(v, SUB, stride=N_VEC), :].astype(f32)
        wet = depth_ref[pl.ds(v, SUB, stride=N_VEC), :] > 0
        cover = jnp.where(wet, ice, zero)
        mass = rows(fields, 2, v) * cover
        strength = rows(fields, 3, v) * cover
        inertia = mass * INV_ICE_STEP
        diag = inertia + WATER_DRAG
        turn = CORIOLIS_PARAM * mass
        inv = 1.0 / (diag * diag + turn * turn)
        half = 0.5 * strength
        half_p.append(half)
        st[0, v] = rows(fields, 0, v)
        st[1, v] = rows(fields, 1, v)
        st[2, v] = half
        st[3, v] = half
        st[4, v] = zero
        cf[0, v] = strength * (2.0**0.5 / 12.0)
        cf[1, v] = inertia
        cf[2, v] = diag * inv
        cf[3, v] = turn * inv
    for v in range(N_VEC):
        half = half_p[v]
        if v:
            below = half_p[v - 1]
        else:
            below = jnp.where(sub == 0, zero, pltpu.roll(half_p[N_VEC - 1], 1, 0))
        west = jnp.where(lane == 0, zero, pltpu.roll(half, 1, 1))
        cf[4, v] = WATER_DRAG * rows(fields, 4, v) - (half - west)
        cf[5, v] = WATER_DRAG * rows(fields, 5, v) - (half - below)


def ice_cycles(tiles, cycles):
    lane, sub = lane_ids(), sub_ids()
    lane_first, lane_last = lane == 0, lane == LANES - 1
    sub_first, sub_last = sub == 0, sub == SUB - 1
    zero = jnp.zeros((SUB, LANES), f32)
    keep = 1.0 / (1.0 + RELAX_RATE)

    def ahead_lane(x):
        return jnp.where(lane_last, zero, pltpu.roll(x, LANES - 1, 1))

    def behind_lane(x):
        return jnp.where(lane_first, zero, pltpu.roll(x, 1, 1))

    def ahead_row(st, i, v):
        if v + 1 < N_VEC:
            return st[i, v + 1]
        return jnp.where(sub_last, zero, pltpu.roll(st[i, 0], SUB - 1, 0))

    def behind_row(st, i, v):
        if v:
            return st[i, v - 1]
        return jnp.where(sub_first, zero, pltpu.roll(st[i, N_VEC - 1], 1, 0))

    def one_cycle(_, carry):
        for st, cf in tiles:
            for v in range(N_VEC):
                u, w = st[0, v], st[1, v]
                ux = ahead_lane(u) - u
                vy = ahead_row(st, 1, v) - w
                shear = (ahead_row(st, 0, v) - u) + (ahead_lane(w) - w)
                both = 1.5 * (ux + vy)
                xx, yy = both + ux, both + vy
                two = (ux * xx + vy * yy) + ((0.5 * shear) * shear + 2.0 * DELTA_FLOOR_SQ)
                k = cf[0, v] * lax.rsqrt(two)
                st[2, v] = keep * st[2, v] + k * xx
                st[3, v] = keep * st[3, v] + k * yy
                st[4, v] = keep * st[4, v] + k * shear
            for v in range(N_VEC):
                u, w = st[0, v], st[1, v]
                sxx, syy, s12 = st[2, v], st[3, v], st[4, v]
                fx = (sxx - behind_lane(sxx)) + (s12 - behind_row(st, 4, v))
                fy = (s12 - behind_lane(s12)) + (syy - behind_row(st, 3, v))
                inertia, ca, cb = cf[1, v], cf[2, v], cf[3, v]
                rx = inertia * u + (fx + cf[4, v])
                ry = inertia * w + (fy + cf[5, v])
                st[0, v] = ca * rx + cb * ry
                st[1, v] = ca * ry - cb * rx
        return carry

    lax.fori_loop(0, cycles, one_cycle, 0)


def ice_finish(st, fields):
    for v in range(N_VEC):
        fields[0, pl.ds(v, SUB, stride=N_VEC), :] = st[0, v]
        fields[1, pl.ds(v, SUB, stride=N_VEC), :] = st[1, v]


def tile_copies(col, refs, fields, mask_v, depth_v, sems):
    vel, mass, strength, mask, depth, ocean = refs
    levels = ocean.shape[0] // 4
    cols = pl.ds(pl.multiple_of(col * TILE, TILE), TILE)
    return [
        pltpu.make_async_copy(vel.at[:, :, cols], fields.at[0:2], sems.at[0]),
        pltpu.make_async_copy(mass.at[:, cols], fields.at[2], sems.at[1]),
        pltpu.make_async_copy(strength.at[:, cols], fields.at[3], sems.at[2]),
        pltpu.make_async_copy(ocean.at[2 * levels, :, cols], fields.at[4], sems.at[3]),
        pltpu.make_async_copy(ocean.at[3 * levels, :, cols], fields.at[5], sems.at[4]),
        pltpu.make_async_copy(mask.at[:, cols], mask_v, sems.at[5]),
        pltpu.make_async_copy(depth.at[:, cols], depth_v, sems.at[6]),
    ]


TILE_COPIES = 7
FIRST_CYCLES = 14
ST_SHAPE, CF_SHAPE = (5, N_VEC, SUB, LANES), (6, N_VEC, SUB, LANES)


def first_ice_kernel(
    owned, vel, mass, strength, mask, depth, ocean, st, cf, fields, mask_v, depth_v, sems
):
    tiles_dev = vel.shape[2] // TILE
    column = owned[0, 0, 0]
    local = jnp.clip(column - lax.axis_index("lon") * tiles_dev, 0, tiles_dev - 1)

    @pl.when(column >= 0)
    def _():
        copies = tile_copies(local, (vel, mass, strength, mask, depth, ocean), fields, mask_v, depth_v, sems)
        for copy in copies:
            copy.start()
        for copy in copies:
            copy.wait()
        ice_prepare(fields, mask_v, depth_v, st, cf)
        ice_cycles([(st, cf)], FIRST_CYCLES)


def first_ice(owned, vel, mass, strength, mask, depth, ocean):
    full = pl.BlockSpec(memory_space=pltpu.VMEM)
    return pl.pallas_call(
        first_ice_kernel,
        out_shape=(jax.ShapeDtypeStruct(ST_SHAPE, f32), jax.ShapeDtypeStruct(CF_SHAPE, f32)),
        in_specs=[SMEM_SPEC] + [ANY] * 6,
        out_specs=(full, full),
        scratch_shapes=[
            pltpu.VMEM((6, TILE, TILE), f32),
            pltpu.VMEM((TILE, TILE), jnp.int32),
            pltpu.VMEM((TILE, TILE), jnp.int32),
            pltpu.SemaphoreType.DMA((TILE_COPIES,)),
        ],
        compiler_params=pltpu.CompilerParams(vmem_limit_bytes=FIRST_VMEM),
        name="ice_first",
    )(owned, vel, mass, strength, mask, depth, ocean)


class Layout:
    def __init__(self, ocean, rows, cols):
        self.levels = ocean // 4
        self.planes = 2 * self.levels
        self.tiles = cols // LANES
        self.fold_depth = self.tiles * self.planes
        self.columns = self.fold_depth + self.tiles
        self.column_fields = self.planes + self.levels + 1
        self.owned = self.columns + 16
        self.size = self.owned + SUB
        self.row_fields = 16


def pack_kernel(
    lay, owned, ocean, depth, piece_out, up_out, down_out, top, top_d, bot, bot_d, west, west_d, east, east_d, tmp, sems
):
    planes, levels, tiles = lay.planes, lay.levels, lay.tiles
    rows, cols = ocean.shape[1], ocean.shape[2]
    n_lon = piece_out.shape[0]
    me = lax.axis_index("lon")
    last = pl.ds(rows - SUB, SUB)
    copies = [
        pltpu.make_async_copy(ocean.at[0:planes, :, 0:LANES], west, sems.at[0]),
        pltpu.make_async_copy(ocean.at[0 : planes + levels, :, cols - LANES : cols], east, sems.at[1]),
        pltpu.make_async_copy(depth.at[:, 0:LANES], west_d, sems.at[2]),
        pltpu.make_async_copy(depth.at[:, cols - LANES : cols], east_d, sems.at[3]),
        pltpu.make_async_copy(ocean.at[:, last, :], top, sems.at[4]),
        pltpu.make_async_copy(depth.at[last, :], top_d, sems.at[5]),
        pltpu.make_async_copy(ocean.at[0:planes, 0:SUB, :], bot, sems.at[6]),
        pltpu.make_async_copy(depth.at[0:SUB, :], bot_d, sems.at[7]),
    ]
    for copy in copies:
        copy.start()
    for copy in copies[:4]:
        copy.wait()
    lane = lane_ids()
    for v in range(rows // SUB):
        at = pl.ds(v * SUB, SUB)
        mixed = jnp.zeros((SUB, LANES), f32)
        for f in range(planes + levels + 1):
            block = east[f, at, :] if f < planes + levels else east_d[at, :].astype(f32)
            mixed = jnp.where(lane == f, pltpu.roll(block, (f + 1) % LANES, 1), mixed)
        for f in range(planes + 1):
            block = west[f, at, :] if f < planes else west_d[at, :].astype(f32)
            mixed = jnp.where(lane == 16 + f, pltpu.roll(block, 16 + f, 1), mixed)
        tmp[at, :] = mixed
    turned = jnp.transpose(tmp[...])
    east_rows, west_rows = turned[0:16], turned[16:32]
    own = jnp.zeros((SUB, LANES), f32)
    for slot in range(owned.shape[2]):
        own = jnp.where(lane == slot, owned[0, 0, slot].astype(f32), own)
    for copy in copies[4:]:
        copy.wait()
    top_rows = jnp.concatenate([top[p, SUB - 1 : SUB, :] for p in range(planes)], axis=0)
    bot_rows = jnp.concatenate([bot[p, 0:1, :] for p in range(planes)], axis=0)
    top_depth = top_d[SUB - 1 : SUB, :].astype(f32)
    up_out[0:planes, :] = top_rows
    for level in range(levels):
        up_out[planes + level : planes + level + 1, :] = top[planes + levels + level, SUB - 1 : SUB, :]
    up_out[planes + levels : planes + levels + 1, :] = top_depth
    down_out[0:planes, :] = bot_rows
    down_out[planes : planes + 1, :] = bot_d[0:1, :].astype(f32)
    for d in range(n_lon):
        for t in range(tiles):
            at = slice(t * LANES, (t + 1) * LANES)
            piece_out[d, t * planes : (t + 1) * planes, :] = top_rows[:, at]
            piece_out[d, lay.fold_depth + t : lay.fold_depth + t + 1, :] = top_depth[:, at]
        eastward = d == lax.rem(me + 1, n_lon)
        piece_out[d, lay.columns : lay.columns + 16, :] = jnp.where(eastward, east_rows, west_rows)
        piece_out[d, lay.owned : lay.owned + SUB, :] = own


def pack(lay, n_lon, owned, ocean, depth):
    rows, cols = ocean.shape[1:]
    full = pl.BlockSpec(memory_space=pltpu.VMEM)
    return pl.pallas_call(
        functools.partial(pack_kernel, lay),
        out_shape=(
            jax.ShapeDtypeStruct((n_lon, lay.size, LANES), f32),
            jax.ShapeDtypeStruct((lay.row_fields, cols), f32),
            jax.ShapeDtypeStruct((lay.row_fields, cols), f32),
        ),
        in_specs=[SMEM_SPEC, ANY, ANY],
        out_specs=(full, full, full),
        scratch_shapes=[
            pltpu.VMEM((4 * lay.levels, SUB, cols), f32),
            pltpu.VMEM((SUB, cols), jnp.int32),
            pltpu.VMEM((lay.planes, SUB, cols), f32),
            pltpu.VMEM((SUB, cols), jnp.int32),
            pltpu.VMEM((lay.planes, rows, LANES), f32),
            pltpu.VMEM((rows, LANES), jnp.int32),
            pltpu.VMEM((lay.planes + lay.levels, rows, LANES), f32),
            pltpu.VMEM((rows, LANES), jnp.int32),
            pltpu.VMEM((rows, LANES), f32),
            pltpu.SemaphoreType.DMA((8,)),
        ],
        name="pack",
    )(owned, ocean, depth)


PART_BLOCKS = 2


def face(lower, upper, vel, shut_above, level):
    quarter = TIME_STEP * vel
    away = jnp.maximum(quarter, 0.0) + TIME_STEP * MIX_HORIZ
    back = quarter - away
    is_open = float(level) < shut_above
    zero = jnp.zeros((SUB, LANES), f32)
    away = jnp.where(is_open, away, zero)
    back = jnp.where(is_open, back, zero)
    return [away * a + back * b for a, b in zip(lower, upper, strict=True)]


def main_kernel(
    lay, n_lon, n_lat, slots,
    partner, owned, ocean, depth, vert, got, from_south, from_north,
    vel, mass, strength, mask, first_st, first_cf,
    out, ice_out,
    cbuf, ubuf, vbuf, mbuf, dint, dbuf, obuf, lists, hal_e, hal_w, gprev,
    all_vel, fields, mask_v, depth_v, tile_sems, st, cf, first_sems, in_sems, out_sems, list_sems, pass_sems,
):
    planes, levels, tiles = lay.planes, lay.levels, lay.tiles
    rows, cols = depth.shape
    blocks = rows // SUB
    me, row_at = lax.axis_index("lon"), lax.axis_index("lat")
    tiles_dev = cols // TILE
    east_dev, west_dev = lax.rem(me + 1, n_lon), lax.rem(me + n_lon - 1, n_lon)

    list_copies = [
        pltpu.make_async_copy(
            got.at[lax.rem(me + slot, n_lon), pl.ds(lay.owned, SUB), :], lists.at[slot - 1], list_sems.at[slot - 1]
        )
        for slot in range(1, slots)
    ]
    for copy in list_copies:
        copy.start()
    start = partner[0]
    source = start // cols
    before = lax.rem(source + n_lon - 1, n_lon)
    in_copies = [
        pltpu.make_async_copy(depth, dint, in_sems.at[0]),
        pltpu.make_async_copy(ocean.at[0:planes], cbuf.at[:, 0:rows, :], in_sems.at[1]),
        pltpu.make_async_copy(ocean.at[planes : planes + levels], ubuf, in_sems.at[2]),
        pltpu.make_async_copy(ocean.at[planes + levels : planes + 2 * levels], vbuf, in_sems.at[3]),
        pltpu.make_async_copy(vert, mbuf, in_sems.at[4]),
        pltpu.make_async_copy(vel, all_vel, in_sems.at[5]),
    ]
    tile_refs = (vel, mass, strength, mask, depth, ocean)
    for copy in list_copies:
        copy.wait()
    columns = [owned[0, 0, 0]] + [lists[slot - 1, 0, slot].astype(jnp.int32) for slot in range(1, slots)]
    listed = [column >= 0 for column in columns]
    local = [jnp.clip(column - me * tiles_dev, 0, tiles_dev - 1) for column in columns]

    def fields_in(slot):
        i = slot - 1
        return tile_copies(local[slot], tile_refs, fields.at[slot], mask_v.at[i], depth_v.at[i], tile_sems.at[slot])

    first_copies = [
        pltpu.make_async_copy(first_st, st.at[0], first_sems.at[0]),
        pltpu.make_async_copy(first_cf, cf.at[0], first_sems.at[1]),
    ]
    for copy in first_copies:
        copy.start()
    for slot in range(1, slots):

        @pl.when(listed[slot])
        def _():
            for copy in fields_in(slot):
                copy.start()

    for copy in in_copies:
        copy.start()
    for slot in range(1, slots):

        @pl.when(listed[slot])
        def _():
            for copy in fields_in(slot):
                copy.wait()
            ice_prepare(fields.at[slot], mask_v.at[slot - 1], depth_v.at[slot - 1], st.at[slot], cf.at[slot])

    for copy in first_copies:
        copy.wait()
    some = functools.reduce(jnp.logical_or, listed)

    @pl.when(some)
    def _():
        every = [(st.at[slot], cf.at[slot]) for slot in range(slots)]
        ice_cycles(every, SUBCYCLES - FIRST_CYCLES)
        ice_cycles(every[1:], FIRST_CYCLES)

    def write_back(slot):
        at = pl.ds(pl.multiple_of(local[slot] * TILE, TILE), TILE)
        return pltpu.make_async_copy(fields.at[slot, 0:2], ice_out.at[:, :, at], tile_sems.at[slot, 0])

    def pass_through(q):
        at = pl.ds(q * TILE, TILE)
        return pltpu.make_async_copy(all_vel.at[:, :, at], ice_out.at[:, :, at], pass_sems.at[q])

    def untouched(q):
        return jnp.logical_not(
            functools.reduce(jnp.logical_or, [on & (at == q) for on, at in zip(listed, local, strict=True)])
        )

    for slot in range(slots):

        @pl.when(listed[slot])
        def _():
            ice_finish(st.at[slot], fields.at[slot])
            write_back(slot).start()

    lane, sub = lane_ids(), sub_ids()
    lane0, lane_last = lane == 0, lane == LANES - 1
    sub0, sub_last = sub == 0, sub == SUB - 1

    pad = jnp.zeros((LANES - 16, LANES), f32)
    hal_e[...] = jnp.transpose(jnp.concatenate([got[east_dev, lay.columns : lay.columns + 16, :], pad], axis=0))
    hal_w[...] = jnp.transpose(jnp.concatenate([got[west_dev, lay.columns : lay.columns + 16, :], pad], axis=0))

    for copy in in_copies:
        copy.wait()
    for q in range(tiles_dev):

        @pl.when(untouched(q))
        def _():
            pass_through(q).start()

    at_top = row_at == n_lat - 1
    offset = lax.rem(start, cols)
    chunk, shift = offset // LANES, lax.rem(offset, LANES)
    index = lax.rem(shift - lane + LANES, LANES)
    from_upper = lane <= shift

    def fold_tile(pos):
        which, tile = jnp.where(pos >= tiles, source, before), lax.rem(pos, tiles)
        tracers = got[which, pl.ds(pl.multiple_of(tile * planes, SUB), planes), :]
        deep = got[which, pl.ds(lay.fold_depth + tile, 1), :]
        return tracers, jnp.broadcast_to(deep, (SUB, LANES))

    for t in range(tiles):
        at = slice(t * LANES, (t + 1) * LANES)
        high, high_d = fold_tile(tiles + chunk - t)
        low, low_d = fold_tile(tiles + chunk - t - 1)
        def pick(a, b):
            return jnp.where(
                from_upper, jnp.take_along_axis(a, index, axis=1), jnp.take_along_axis(b, index, axis=1)
            )
        north = jnp.where(at_top, pick(high, low), from_north[0:planes, at])
        north_d = jnp.where(at_top, pick(high_d, low_d), from_north[planes : planes + 1, at])
        for p in range(planes):
            cbuf[p, rows : rows + SUB, at] = jnp.broadcast_to(north[p : p + 1], (SUB, LANES))
        dbuf[rows : rows + SUB, at] = north_d
    for b in range(blocks):
        dbuf[b * SUB : (b + 1) * SUB, :] = dint[b * SUB : (b + 1) * SUB, :].astype(f32)

    def tracers_of(level):
        return (level, levels + level)

    not_bottom = row_at > 0
    for t in range(tiles):
        at = slice(t * LANES, (t + 1) * LANES)
        deep = jnp.where(not_bottom, from_south[planes + levels : planes + levels + 1, at], 0.0)
        shut = jnp.minimum(jnp.broadcast_to(deep, (SUB, LANES)), north_of(dbuf[0:SUB, at], dbuf[0:SUB, at], sub0))
        for level in range(levels):
            lower = [jnp.broadcast_to(from_south[p : p + 1, at], (SUB, LANES)) for p in tracers_of(level)]
            upper = [north_of(cbuf[p, 0:SUB, at], cbuf[p, 0:SUB, at], sub0) for p in tracers_of(level)]
            speed = jnp.broadcast_to(from_south[planes + level : planes + level + 1, at], (SUB, LANES))
            for p, g in zip(tracers_of(level), face(lower, upper, speed, shut, level), strict=True):
                gprev[p, :, at] = g

    zero = jnp.zeros((SUB, LANES), f32)

    def one_block(b, carry):
        r0 = pl.multiple_of(b * SUB, SUB)
        here, ahead = pl.ds(r0, SUB), pl.ds(pl.multiple_of(r0 + SUB, SUB), SUB)
        side_e, side_w = hal_e[here, :], hal_w[here, :]

        def load_c(t):
            at = slice(t * LANES, (t + 1) * LANES)
            return [cbuf[p, here, at] for p in range(planes)]

        cur, cur_d = load_c(0), dbuf[here, 0:LANES]
        shut = jnp.minimum(pltpu.roll(side_w, (LANES - 1 - (planes + levels)) % LANES, 1), pltpu.roll(cur_d, LANES - 1, 1))
        g_prev = [None] * planes
        for level in range(levels):
            lower = [pltpu.roll(side_w, LANES - 1 - p, 1) for p in tracers_of(level)]
            upper = [pltpu.roll(cur[p], LANES - 1, 1) for p in tracers_of(level)]
            speed = pltpu.roll(side_w, LANES - 1 - (planes + level), 1)
            for p, g in zip(tracers_of(level), face(lower, upper, speed, shut, level), strict=True):
                g_prev[p] = g
        for t in range(tiles):
            at = slice(t * LANES, (t + 1) * LANES)
            if t + 1 < tiles:
                nxt, nxt_d = load_c(t + 1), dbuf[here, (t + 1) * LANES : (t + 2) * LANES]
            else:
                nxt = [pltpu.roll(side_e, (LANES - p) % LANES, 1) for p in range(planes)]
                nxt_d = pltpu.roll(side_e, LANES - planes, 1)
            shut_e = jnp.minimum(cur_d, east_of(cur_d, nxt_d, lane0))
            shut_n = jnp.minimum(cur_d, north_of(cur_d, dbuf[ahead, at], sub0))
            interim = [None] * planes
            for level in range(levels):
                pair = tracers_of(level)
                lower = [cur[p] for p in pair]
                east = [east_of(cur[p], nxt[p], lane0) for p in pair]
                north = [north_of(cur[p], cbuf[p, ahead, at], sub0) for p in pair]
                g_east = face(lower, east, ubuf[level, here, at], shut_e, level)
                g_north = face(lower, north, vbuf[level, here, at], shut_n, level)
                for p, c, ge, gn in zip(pair, lower, g_east, g_north, strict=True):
                    g_west = west_of(ge, g_prev[p], lane_last)
                    g_south = south_of(gn, gprev[p, :, at], sub_last)
                    gprev[p, :, at] = gn
                    g_prev[p] = ge
                    interim[p] = c - ((ge - g_west) + (gn - g_south))
            mix = [
                jnp.where(float(level) < cur_d, TIME_STEP * mbuf[level, here, at], zero) for level in range(levels)
            ]
            ratio = [None] * levels
            solved = [None] * planes
            y = [[None] * levels, [None] * levels]
            for level in range(levels):
                diag = mix[level] + 1.0
                if level + 1 < levels:
                    diag = diag + mix[level + 1]
                if level:
                    ratio[level] = mix[level] * inv
                    diag = diag - mix[level] * ratio[level]
                inv = 1.0 / diag
                for tracer in range(2):
                    rhs = interim[tracer * levels + level]
                    if level:
                        rhs = rhs + mix[level] * y[tracer][level - 1]
                    y[tracer][level] = rhs * inv
            for tracer in range(2):
                z = y[tracer][levels - 1]
                obuf[tracer * levels + levels - 1, here, at] = z
                for level in range(levels - 2, -1, -1):
                    z = y[tracer][level] + ratio[level + 1] * z
                    obuf[tracer * levels + level, here, at] = z
            cur, cur_d = nxt, nxt_d
        return carry

    parts = out_sems.shape[0]
    per = blocks // parts

    def out_copy(part):
        at = pl.ds(pl.multiple_of(part * per * SUB, per * SUB), per * SUB)
        return pltpu.make_async_copy(obuf.at[:, at, :], out.at[:, at, :], out_sems.at[part])

    def one_part(part, carry):
        lax.fori_loop(part * per, (part + 1) * per, one_block, 0)
        out_copy(part).start()
        return carry

    lax.fori_loop(0, parts, one_part, 0)
    for slot in range(slots):

        @pl.when(listed[slot])
        def _():
            write_back(slot).wait()

    for q in range(tiles_dev):

        @pl.when(untouched(q))
        def _():
            pass_through(q).wait()

    for part in range(parts):
        out_copy(part).wait()


def main(lay, n_lon, n_lat, partner, owned, ocean, depth, vert, got, south, north, vel, mass, strength, mask, first):
    rows, cols = depth.shape
    levels, planes = lay.levels, lay.planes
    slots = owned.shape[2]
    full = pl.BlockSpec(memory_space=pltpu.VMEM)
    return pl.pallas_call(
        functools.partial(main_kernel, lay, n_lon, n_lat, slots),
        out_shape=(
            jax.ShapeDtypeStruct((planes, rows, cols), f32),
            jax.ShapeDtypeStruct(vel.shape, f32),
        ),
        in_specs=[SMEM_SPEC, SMEM_SPEC] + [ANY] * 3 + [full] * 3 + [ANY] * 6,
        out_specs=(ANY, ANY),
        scratch_shapes=[
            pltpu.VMEM((planes, rows + SUB, cols), f32),
            pltpu.VMEM((levels, rows, cols), f32),
            pltpu.VMEM((levels, rows, cols), f32),
            pltpu.VMEM((levels, rows, cols), f32),
            pltpu.VMEM((rows, cols), jnp.int32),
            pltpu.VMEM((rows + SUB, cols), f32),
            pltpu.VMEM((planes, rows, cols), f32),
            pltpu.SMEM((slots - 1, SUB, LANES), f32),
            pltpu.VMEM((rows, LANES), f32),
            pltpu.VMEM((rows, LANES), f32),
            pltpu.VMEM((planes, SUB, cols), f32),
            pltpu.VMEM(vel.shape, f32),
            pltpu.VMEM((slots, 6, TILE, TILE), f32),
            pltpu.VMEM((slots - 1, TILE, TILE), jnp.int32),
            pltpu.VMEM((slots - 1, TILE, TILE), jnp.int32),
            pltpu.SemaphoreType.DMA((slots, TILE_COPIES)),
            pltpu.VMEM((slots, *ST_SHAPE), f32),
            pltpu.VMEM((slots, *CF_SHAPE), f32),
            pltpu.SemaphoreType.DMA((2,)),
            pltpu.SemaphoreType.DMA((6,)),
            pltpu.SemaphoreType.DMA((rows // (PART_BLOCKS * SUB),)),
            pltpu.SemaphoreType.DMA((slots - 1,)),
            pltpu.SemaphoreType.DMA((cols // TILE,)),
        ],
        compiler_params=pltpu.CompilerParams(vmem_limit_bytes=MAIN_VMEM),
        name="main",
    )(partner, owned, ocean, depth, vert, got, south, north, vel, mass, strength, mask, *first)


def on_device(
    ocean_state,
    depth_levels,
    vert_mix,
    partner,
    ice_velocity,
    ice_mass,
    ice_strength,
    ice_mask,
    ice_owned,
):
    n_lon, n_lat = lax.axis_size("lon"), lax.axis_size("lat")
    fields, levels, rows, cols = ocean_state.shape
    ocean = ocean_state.reshape(fields * levels, rows, cols)
    lay = Layout(fields * levels, rows, cols)
    piece, up, down = pack(lay, n_lon, ice_owned, ocean, depth_levels)
    got = lax.all_to_all(piece, "lon", 0, 0, tiled=True)
    south = lax.ppermute(up, "lat", [(i, i + 1) for i in range(n_lat - 1)])
    north = lax.ppermute(down, "lat", [(i + 1, i) for i in range(n_lat - 1)])
    first = first_ice(ice_owned, ice_velocity, ice_mass, ice_strength, ice_mask, depth_levels, ocean)
    tracers, ice = main(
        lay, n_lon, n_lat, partner, ice_owned, ocean, depth_levels, vert_mix, got, south, north,
        ice_velocity, ice_mass, ice_strength, ice_mask, first,
    )
    return tracers.reshape(2, levels, rows, cols), ice


def solution(mesh):
    return jax.shard_map(
        on_device,
        mesh=mesh,
        in_specs=(
            P(None, None, "lat", "lon"),
            P("lat", "lon"),
            P(None, "lat", "lon"),
            P("lon"),
            P(None, "lat", "lon"),
            P("lat", "lon"),
            P("lat", "lon"),
            P("lat", "lon"),
            P("lat", "lon", None),
        ),
        out_specs=(P(None, None, "lat", "lon"), P(None, "lat", "lon")),
        check_vma=False,
    )
```
